32 devices in a mesh: rep: 4 (over y, x), fsdp: 4 (over z), tp: 2 (over core).
Axes of the slice: x: 2, y: 2, z: 4, core: 2. Of those that a mesh axis runs over, the one named last changes fastest.
Arguments:
- tokens: bfloat16 [4096, 8192], P(('rep', 'fsdp'), 'tp'), may hold values from -6 to 6
- cotangent: bfloat16 [4096, 512], P(('rep', 'fsdp'), 'tp'), may hold values from -6 to 6
- weight: bfloat16 [512, 8192], P('fsdp', 'tp'), may hold values from -0.0625 to 0.0625
- momentum: bfloat16 [4, 512, 8192], P('rep', 'fsdp', 'tp'), may hold values from -6 to 6
Outputs:
- projected: bfloat16 [4096, 512], P(('rep', 'fsdp'))
- update: float32 [512, 8192], P('fsdp', 'tp')
- momentum_out: float32 [4, 512, 8192], P('rep', 'fsdp', 'tp')
The draws below stay inside these ranges and needn't reach their ends.
All inputs are finite; a program needn't handle non-finite values.
Results may differ from the reference program's by a relative error of at most 0.006.
Values may be sent and summed in bfloat16 or wider, within the bound.
A program may use at most 64 MiB of HBM per device.

```python
import math
import jax
import jax.numpy as jnp
from jax import lax

D = 8192
COLS = 512
TOK_DEV = 256
TOKENS = 4096
N_REP = 4
N_FSDP = 4


def strengthened(array, key, source, target, shards_of, factor):
    def block_of(dim):
        return (jnp.arange(array.shape[dim]) // (array.shape[dim] // shards_of)).reshape((-1,) + (1,) * (array.ndim - 1 - dim))

    first = jax.random.permutation(key, shards_of)[block_of(target)]
    other_side = (block_of(target) + shards_of // 2) % shards_of
    return jnp.where((block_of(source) == first) | (block_of(source) == other_side), factor * array, array)


def levels(own_key, shape, split, low, largest):
    factor_of, own = 1.0, jax.random.fold_in(own_key, 6)
    for axis_at, shards_of in split:
        draws = jnp.exp(jax.random.uniform(jax.random.fold_in(own, axis_at), (shards_of,), jnp.float32, low / len(split), largest / len(split)))
        factor_of = factor_of * jnp.repeat(draws, shape[axis_at] // shards_of).reshape([-1 if axis == axis_at else 1 for axis in range(len(shape))])
    return factor_of


def scatter_about(stream_key, shape, width, most, shards=(), held_as=jnp.bfloat16):
    array = jax.random.normal(stream_key, shape, jnp.float32) * width
    if len(shards) > 0:
        array = levels(stream_key, shape, shards, -0.22, 0.18) * array
    return jnp.clip(array, min=-most, max=most).astype(held_as)


def heavy_noise(own_key, dims, spread, most, shards, heavy, dtype=jnp.bfloat16):
    entries = spread * jax.random.normal(own_key, dims, jnp.float32)
    if shards:
        entries = entries * levels(own_key, dims, shards, -0.22, 0.18)
    return jnp.clip(strengthened(entries, jax.random.fold_in(own_key, 3), *heavy), -most, most).astype(dtype)


def setup_inputs(seed: int = 0) -> dict:
    key_list = jax.random.split(jax.random.key(seed), 5)
    tokens = scatter_about(key_list[0], (TOKENS, D), 1.0, 6.0, ((0, 16), (1, 2)))
    cotangent = heavy_noise(key_list[1], (TOKENS, COLS), 1.0, 6.0, ((0, 16), (1, 2)), (0, 1, 16, 2.0))
    weight = scatter_about(key_list[2], (COLS, D), D ** -0.5, 0.0625, ((0, 4), (1, 2)))
    momentum = scatter_about(key_list[3], (N_REP, COLS, D), 1.0, 6.0, ((0, 4), (1, 4), (2, 2)))
    return dict(tokens=tokens, cotangent=cotangent, weight=weight, momentum=momentum)


BETA_ONE = 0.9
BETA_TWO = 0.99
SOFT_WIDTH = 0.25

def reference(tokens, cotangent, weight, momentum):
    projected = jnp.dot(tokens, weight.T, preferred_element_type=jnp.float32).astype(jnp.bfloat16)
    scale = 1.0 / math.sqrt(TOK_DEV * N_FSDP)
    token_blocks = tokens.reshape(N_REP, N_FSDP, TOK_DEV, D)
    cot_blocks = cotangent.reshape(N_REP, N_FSDP, TOK_DEV, COLS)

    def shard_term(running, inputs):
        rows, cots = inputs
        partial_term = jnp.dot(cots.T, rows, preferred_element_type=jnp.float32).astype(jnp.bfloat16)
        partial_term = lax.optimization_barrier(partial_term)
        return (running + partial_term.astype(jnp.float32), None)

    def replica(tally, inputs):
        rows, cots, moment_in = inputs
        gradient, _ = lax.scan(shard_term, jnp.zeros((COLS, D), jnp.float32), (rows, cots))
        gradient = gradient * scale
        moment = moment_in.astype(jnp.float32)
        blended = BETA_ONE * moment + (1.0 - BETA_ONE) * gradient
        soft_sign = jnp.clip(blended / SOFT_WIDTH, -1.0, 1.0)
        renewed = BETA_TWO * moment + (1.0 - BETA_TWO) * gradient
        return (tally + soft_sign, renewed)
    tally, momentum_out = lax.scan(replica, jnp.zeros((COLS, D), jnp.float32), (token_blocks, cot_blocks, momentum))
    update = jnp.clip(tally, -1.0, 1.0)
    return (projected, update, momentum_out)
```

```python
import functools
import math

import jax
import jax.numpy as jnp
from jax import lax
from jax.experimental import pallas as pl
from jax.experimental.pallas import tpu as pltpu
from jax.sharding import PartitionSpec as P

BETA_ONE = 0.9
BETA_TWO = 0.99
SOFT_WIDTH = 0.25
LANES = 128
MESH = pl.DeviceIdType.MESH
F32 = jnp.float32
BF16 = jnp.bfloat16


def step(dims, scale, tok, cot, wgt, mom, proj, upd, grad, *scratch):
    (n, nrep, ntp, pieces, rows, width, share) = dims
    (right_buf, left_buf, part, weights, cots, halves, signs, votes, tally) = scratch[:9]
    (rs_s, rs_r, ls_s, ls_r, wrs, wrr, wls, wlr, wps, wpr, vs, vr, ts, tr, cs, cr, hs, hr) = scratch[9:]
    z, me, t = lax.axis_index("fsdp"), lax.axis_index("rep"), lax.axis_index("tp")
    quarter = weights.shape[1] // nrep
    tp_cols = cot.shape[1]

    def to(axis, at):
        return dict(device_id={axis: at}, device_id_type=MESH)

    def other(off, size, at):
        return lax.rem(at + off, size)

    barrier = pltpu.get_barrier_semaphore()
    for axis, at, size in (("tp", t, ntp), ("rep", me, nrep)):
        for off in range(1, size):
            pl.semaphore_signal(barrier, inc=1, **to(axis, other(off, size, at)))
    for off in (1, n - 1):
        pl.semaphore_signal(barrier, inc=1, **to("fsdp", other(off, n, z)))
    pl.semaphore_wait(barrier, ntp + nrep)

    def cot_copy(off):
        return pltpu.make_async_remote_copy(
            cot, cots.at[t], cs.at[off], cr.at[off], **to("tp", other(off, ntp, t)))

    def half_copy(off):
        return pltpu.make_async_remote_copy(
            halves.at[t], halves.at[t], hs.at[off], hr.at[off], **to("tp", other(off, ntp, t)))

    def weight_slot(shard, rep):
        return weights.at[pl.ds(pl.multiple_of(shard * rows, rows), rows),
                          pl.ds(pl.multiple_of(rep * quarter, LANES), quarter)]

    def weight_line(own, shard, send, recv, target):
        slot = weight_slot(shard, me)
        source = wgt.at[:, pl.ds(pl.multiple_of(me * quarter, LANES), quarter)] if own else slot
        return pltpu.make_async_remote_copy(
            source, slot, send.at[shard], recv.at[shard], **to("fsdp", target))

    def weight_plane(shard, off):
        slot = weight_slot(shard, me)
        return pltpu.make_async_remote_copy(
            slot, slot, wps.at[shard, off], wpr.at[shard, off], **to("rep", other(off, nrep, me)))

    def sum_copy(buf, p, k, send, recv, target):
        slot = buf.at[p, pl.ds(pl.multiple_of(k * rows, rows), rows), :]
        return pltpu.make_async_remote_copy(slot, slot, send.at[p, k], recv.at[p, k], **to("fsdp", target))

    def vote_copy(p, off):
        return pltpu.make_async_remote_copy(
            signs.at[p, other(off, nrep, me)], votes.at[p, me], vs.at[p, off], vr.at[p, off],
            **to("rep", other(off, nrep, me)))

    def tally_copy(p, off):
        return pltpu.make_async_remote_copy(
            tally.at[p, me], tally.at[p, me], ts.at[p, off], tr.at[p, off],
            **to("rep", other(off, nrep, me)))

    def weight_step(i):
        for send, recv, shard, target, ok in (
            (wrs, wrr, z - i, z + 1, z + 1 < n), (wls, wlr, z + i, z - 1, z > 0)):
            here = (shard >= 0) & (shard < n)
            if i > 0:
                @pl.when(here)
                def _():
                    weight_line(False, shard, send, recv, z).wait_recv()
            @pl.when(here & ok)
            def _():
                weight_line(i == 0, shard, send, recv, target).start()
            if i > 0:
                @pl.when(here)
                def _():
                    for off in range(1, nrep):
                        weight_plane(shard, off).start()

    def sum_step(tau):
        for buf, send, recv, i, first, toward, left in (
            (right_buf, rs_s, rs_r, tau - z, z == 0, z + 1, False),
            (left_buf, ls_s, ls_r, tau - (n - 1 - z), z == n - 1, z - 1, True)):
            p, j = i // (n - 1), lax.rem(jnp.maximum(i, 0), n - 1)
            k = j if left else n - 1 - j
            inside = (i >= 0) & (i < pieces * (n - 1))
            ahead = (k < z) if left else (k > z)
            @pl.when(inside & (ahead | (k == z)) & jnp.logical_not(first))
            def _():
                sum_copy(buf, p, k, send, recv, z).wait_recv()
            rk = pl.ds(pl.multiple_of(k * rows, rows), rows)
            @pl.when(inside & ahead & first)
            def _():
                buf[p, rk, :] = part[p, rk, :]
            @pl.when(inside & ahead & jnp.logical_not(first))
            def _():
                buf[p, rk, :] = (buf[p, rk, :].astype(F32) + part[p, rk, :].astype(F32)).astype(BF16)
            @pl.when(inside & ahead)
            def _():
                sum_copy(buf, p, k, send, recv, toward).start()

    own_rows = pl.ds(pl.multiple_of(z * rows, rows), rows)

    def vote(p):
        for s in range(nrep):
            cut = pl.ds(s * share, share)
            at = pl.ds(p * width + s * share, share)
            g = (part[p, own_rows, cut].astype(F32) + right_buf[p, own_rows, cut].astype(F32)
                 + left_buf[p, own_rows, cut].astype(F32)) * scale
            grad[:, at] = g.astype(BF16)
            blended = BETA_ONE * mom[0, :, at].astype(F32) + (1.0 - BETA_ONE) * g
            signs[p, s] = jnp.clip(blended / SOFT_WIDTH, -1.0, 1.0).astype(BF16)
        for off in range(1, nrep):
            vote_copy(p, off).start()

    def count(p):
        total = signs[p, me].astype(F32)
        for off in range(1, nrep):
            vote_copy(p, off).wait_recv()
            total = total + votes[p, other(nrep - off, nrep, me)].astype(F32)
        tally[p, me] = jnp.clip(total, -1.0, 1.0).astype(BF16)
        for off in range(1, nrep):
            tally_copy(p, off).start()

    def finish(p):
        for off in range(1, nrep):
            tally_copy(p, off).wait_recv()
        for s in range(nrep):
            upd[:, pl.ds(p * width + s * share, share)] = tally[p, s]

    def project():
        for i in range(n):
            for shard in ((z - i, z + i) if i > 0 else ()):
                @pl.when((shard >= 0) & (shard < n))
                def _():
                    for off in range(1, nrep):
                        weight_plane(shard, off).wait_recv()
        halves[t] = jnp.zeros(halves.shape[1:], F32)
        @pl.loop(0, pieces)
        def _(p):
            at = pl.ds(pl.multiple_of(p * width, LANES), width)
            halves[t] += lax.dot_general(
                tok[:, at], weights[:, at], (((1,), (1,)), ((), ())), preferred_element_type=F32)
        for off in range(1, ntp):
            half_copy(off).start()

    for off in range(1, ntp):
        cot_copy(off).start()
    weight_step(0)
    weights[own_rows, :] = wgt[...]
    cots[t] = cot[...]
    for buf, edge in ((right_buf, 0), (left_buf, n - 1)):
        @pl.when(z == edge)
        def _():
            buf[:, edge * rows:(edge + 1) * rows, :] = jnp.zeros((pieces, rows, width), BF16)
    for off in range(1, ntp):
        cot_copy(off).wait_recv()

    @pl.loop(0, pieces)
    def _(p):
        at = pl.ds(pl.multiple_of(p * width, LANES), width)
        for b in range(ntp):
            part[p, b * tp_cols:(b + 1) * tp_cols, :] = lax.dot_general(
                cots[b], tok[:, at], (((0,), (0,)), ((), ())), preferred_element_type=F32).astype(BF16)

    last = pieces * (n - 1)
    for tau in range(last + 1):
        if 0 < tau < n:
            weight_step(tau)
        sum_step(tau)
        p, j = tau // (n - 1), tau % (n - 1)
        if j == 0 and p > 0:
            vote(p - 1)
        if j == (n - 1) // 2 + (n > 3) and 0 < p < pieces:
            count(p - 1)
        if tau == last:
            project()
    count(pieces - 1)
    for off in range(1, ntp):
        half_copy(off).wait_recv()
    total = halves[0]
    for b in range(1, ntp):
        total = total + halves[b]
    proj[...] = total.astype(BF16)
    for p in range(pieces):
        finish(p)

    for off in range(1, ntp):
        cot_copy(off).wait_send()
        half_copy(off).wait_send()
    for p in range(pieces):
        for off in range(1, nrep):
            vote_copy(p, off).wait_send()
            tally_copy(p, off).wait_send()
        for k in range(n):
            @pl.when(k > z)
            def _():
                sum_copy(right_buf, p, k, rs_s, rs_r, z).wait_send()
            @pl.when(k < z)
            def _():
                sum_copy(left_buf, p, k, ls_s, ls_r, z).wait_send()
    for shard in range(n):
        @pl.when((shard <= z) & (z + 1 < n))
        def _():
            weight_line(False, shard, wrs, wrr, z).wait_send()
        @pl.when((shard >= z) & (z > 0))
        def _():
            weight_line(False, shard, wls, wlr, z).wait_send()
        @pl.when(shard != z)
        def _():
            for off in range(1, nrep):
                weight_plane(shard, off).wait_send()


def shards(n, nrep, ntp, tokens, cotangent, weight, momentum):
    held, half = tokens.shape
    rows, cols = weight.shape[0], weight.shape[0] * n
    pieces = max(1, min(4, half // (LANES * nrep)))
    width = half // pieces
    share = width // nrep
    scale = 1.0 / math.sqrt(held * n)
    dma = pltpu.SemaphoreType.DMA
    vmem = pl.BlockSpec(memory_space=pltpu.VMEM)
    projected, update, gradient = pl.pallas_call(
        functools.partial(step, (n, nrep, ntp, pieces, rows, width, share), scale),
        out_shape=(
            jax.ShapeDtypeStruct((held, cols), BF16),
            jax.ShapeDtypeStruct((rows, half), BF16),
            jax.ShapeDtypeStruct((rows, half), BF16),
        ),
        in_specs=[vmem] * 4,
        out_specs=(vmem,) * 3,
        scratch_shapes=[
            pltpu.VMEM((pieces, cols, width), BF16),
            pltpu.VMEM((pieces, cols, width), BF16),
            pltpu.VMEM((pieces, cols, width), BF16),
            pltpu.VMEM((cols, half), BF16),
            pltpu.VMEM((ntp,) + cotangent.shape, BF16),
            pltpu.VMEM((ntp, held, cols), F32),
            pltpu.VMEM((pieces, nrep, rows, share), BF16),
            pltpu.VMEM((pieces, nrep, rows, share), BF16),
            pltpu.VMEM((pieces, nrep, rows, share), BF16),
        ]
        + [dma((pieces, n))] * 4
        + [dma((n,))] * 4
        + [dma((n, nrep))] * 2
        + [dma((pieces, nrep))] * 4
        + [dma((ntp,))] * 4,
        compiler_params=pltpu.CompilerParams(
            collective_id=0, has_side_effects=True, vmem_limit_bytes=60 * 1024 * 1024
        ),
    )(tokens, cotangent, weight, momentum)
    renewed = BETA_TWO * momentum.astype(F32) + (1.0 - BETA_TWO) * gradient.astype(F32)[None]
    return (projected, update.astype(F32), renewed)


def solution(mesh):
    sizes = dict(mesh.shape)
    return jax.shard_map(
        functools.partial(shards, sizes["fsdp"], sizes["rep"], sizes["tp"]),
        mesh=mesh,
        in_specs=(
            P(("rep", "fsdp"), "tp"),
            P(("rep", "fsdp"), "tp"),
            P("fsdp", "tp"),
            P("rep", "fsdp", "tp"),
        ),
        out_specs=(P(("rep", "fsdp"), None), P("fsdp", "tp"), P("rep", "fsdp", "tp")),
        check_vma=False,
    )
```

```python
import functools
import math

import jax
import jax.numpy as jnp
from jax import lax
from jax.experimental import pallas as pl
from jax.experimental.pallas import tpu as pltpu
from jax.sharding import PartitionSpec as P

BETA_ONE = 0.9
BETA_TWO = 0.99
SOFT_WIDTH = 0.25
LANES = 128
MESH = pl.DeviceIdType.MESH
F32 = jnp.float32
BF16 = jnp.bfloat16


def step(dims, scale, tok, cot, wgt, mom, proj, upd, grad, *scratch):
    (n, nrep, ntp, pieces, rows, width, share) = dims
    (right_buf, left_buf, part, weights, cots, halves, signs, votes, tally, edge_toks, edge_cots) = scratch[:11]
    (rs_s, rs_r, ls_s, ls_r, wrs, wrr, wls, wlr, wps, wpr, vs, vr, ts, tr, cs, cr, hs, hr, es, er) = scratch[11:]
    z, me, t = lax.axis_index("fsdp"), lax.axis_index("rep"), lax.axis_index("tp")
    quarter = weights.shape[1] // nrep
    tp_cols = cot.shape[1]

    def to(axis, at):
        return dict(device_id={axis: at}, device_id_type=MESH)

    def other(off, size, at):
        return lax.rem(at + off, size)

    barrier = pltpu.get_barrier_semaphore()
    for axis, at, size in (("tp", t, ntp), ("rep", me, nrep)):
        for off in range(1, size):
            pl.semaphore_signal(barrier, inc=1, **to(axis, other(off, size, at)))
    for off in (1, n - 1):
        pl.semaphore_signal(barrier, inc=1, **to("fsdp", other(off, n, z)))
    pl.semaphore_wait(barrier, ntp + nrep)

    def cot_copy(off):
        return pltpu.make_async_remote_copy(
            cot, cots.at[t], cs.at[off], cr.at[off], **to("tp", other(off, ntp, t)))

    def half_copy(off):
        return pltpu.make_async_remote_copy(
            halves.at[t], halves.at[t], hs.at[off], hr.at[off], **to("tp", other(off, ntp, t)))

    def weight_slot(shard, rep):
        return weights.at[pl.ds(pl.multiple_of(shard * rows, rows), rows),
                          pl.ds(pl.multiple_of(rep * quarter, LANES), quarter)]

    def weight_line(own, shard, send, recv, target):
        slot = weight_slot(shard, me)
        source = wgt.at[:, pl.ds(pl.multiple_of(me * quarter, LANES), quarter)] if own else slot
        return pltpu.make_async_remote_copy(
            source, slot, send.at[shard], recv.at[shard], **to("fsdp", target))

    def weight_plane(shard, off):
        slot = weight_slot(shard, me)
        return pltpu.make_async_remote_copy(
            slot, slot, wps.at[shard, off], wpr.at[shard, off], **to("rep", other(off, nrep, me)))

    def sum_copy(buf, p, k, send, recv, target):
        slot = buf.at[p, pl.ds(pl.multiple_of(k * rows, rows), rows), :]
        return pltpu.make_async_remote_copy(slot, slot, send.at[p, k], recv.at[p, k], **to("fsdp", target))

    def edge_cot_copy(side, target):
        return pltpu.make_async_remote_copy(
            cots, edge_cots.at[side], es.at[side, pieces], er.at[side, pieces], **to("fsdp", target))

    def edge_tok_copy(side, p, target):
        at = pl.ds(pl.multiple_of(p * width, LANES), width)
        return pltpu.make_async_remote_copy(
            tok.at[:, at], edge_toks.at[side, p], es.at[side, p], er.at[side, p], **to("fsdp", target))

    def vote_copy(p, off):
        return pltpu.make_async_remote_copy(
            signs.at[p, other(off, nrep, me)], votes.at[p, me], vs.at[p, off], vr.at[p, off],
            **to("rep", other(off, nrep, me)))

    def tally_copy(p, off):
        return pltpu.make_async_remote_copy(
            tally.at[p, me], tally.at[p, me], ts.at[p, off], tr.at[p, off],
            **to("rep", other(off, nrep, me)))

    def weight_step(i, first=False):
        for send, recv, shard, target, ok in (
            (wrs, wrr, z - i, z + 1, z + 1 < n), (wls, wlr, z + i, z - 1, z > 0)):
            here = (shard >= 0) & (shard < n)
            if not first:
                @pl.when(here)
                def _():
                    weight_line(False, shard, send, recv, z).wait_recv()
            @pl.when(here & ok)
            def _():
                weight_line(first, shard, send, recv, target).start()
            if not first:
                @pl.when(here)
                def _():
                    for off in range(1, nrep):
                        weight_plane(shard, off).start()

    def sum_step(tau):
        for side, buf, send, recv, depth, toward in (
            (0, right_buf, rs_s, rs_r, z, z + 1), (1, left_buf, ls_s, ls_r, n - 1 - z, z - 1)):
            i = tau - depth
            p, j = i // (n - 1), lax.rem(jnp.maximum(i, 0), n - 1)
            k = j if side else n - 1 - j
            inside = (i >= 0) & (i < pieces * (n - 1))
            ahead = (k < z) if side else (k > z)
            @pl.when(inside & (depth == 1) & (j == 0))
            def _():
                @pl.when(p == 0)
                def _():
                    edge_cot_copy(side, z).wait_recv()
                edge_tok_copy(side, p, z).wait_recv()
                for b in range(ntp):
                    buf[p, b * tp_cols:(b + 1) * tp_cols, :] = lax.dot_general(
                        edge_cots[side, b], edge_toks[side, p], (((0,), (0,)), ((), ())),
                        preferred_element_type=F32).astype(BF16)
            @pl.when(inside & (ahead | (k == z)) & (depth > 1))
            def _():
                sum_copy(buf, p, k, send, recv, z).wait_recv()
            rk = pl.ds(pl.multiple_of(k * rows, rows), rows)
            @pl.when(inside & ahead & (depth > 0))
            def _():
                buf[p, rk, :] = (buf[p, rk, :].astype(F32) + part[p, rk, :].astype(F32)).astype(BF16)
                sum_copy(buf, p, k, send, recv, toward).start()

    own_rows = pl.ds(pl.multiple_of(z * rows, rows), rows)

    def vote(p):
        for s in range(nrep):
            cut = pl.ds(s * share, share)
            at = pl.ds(pl.multiple_of(p * width + s * share, LANES), share)
            g = (part[p, own_rows, cut].astype(F32) + right_buf[p, own_rows, cut].astype(F32)
                 + left_buf[p, own_rows, cut].astype(F32)) * scale
            grad[:, at] = g.astype(BF16)
            blended = BETA_ONE * mom[0, :, at].astype(F32) + (1.0 - BETA_ONE) * g
            signs[p, s] = jnp.clip(blended / SOFT_WIDTH, -1.0, 1.0).astype(BF16)
        for off in range(1, nrep):
            vote_copy(p, off).start()

    def count(p):
        total = signs[p, me].astype(F32)
        for off in range(1, nrep):
            vote_copy(p, off).wait_recv()
            total = total + votes[p, other(nrep - off, nrep, me)].astype(F32)
        tally[p, me] = jnp.clip(total, -1.0, 1.0).astype(BF16)
        for off in range(1, nrep):
            tally_copy(p, off).start()

    def finish(p):
        for off in range(1, nrep):
            tally_copy(p, off).wait_recv()
        for s in range(nrep):
            upd[:, pl.ds(pl.multiple_of(p * width + s * share, LANES), share)] = tally[p, s]

    def project():
        for i in range(n):
            for shard in ((z - i, z + i) if i > 0 else ()):
                @pl.when((shard >= 0) & (shard < n))
                def _():
                    for off in range(1, nrep):
                        weight_plane(shard, off).wait_recv()
        halves[t] = jnp.zeros(halves.shape[1:], F32)
        @pl.loop(0, pieces)
        def _(p):
            at = pl.ds(pl.multiple_of(p * width, LANES), width)
            halves[t] += lax.dot_general(
                tok[:, at], weights[:, at], (((1,), (1,)), ((), ())), preferred_element_type=F32)
        for off in range(1, ntp):
            half_copy(off).start()

    for off in range(1, ntp):
        cot_copy(off).start()
    weight_step(0, True)
    weights[own_rows, :] = wgt[...]
    cots[t] = cot[...]
    for buf, edge in ((right_buf, 0), (left_buf, n - 1)):
        @pl.when(z == edge)
        def _():
            buf[:, edge * rows:(edge + 1) * rows, :] = jnp.zeros((pieces, rows, width), BF16)
    for off in range(1, ntp):
        cot_copy(off).wait_recv()
    for side, edge, target in ((0, 0, z + 1), (1, n - 1, z - 1)):
        @pl.when(z == edge)
        def _():
            edge_cot_copy(side, target).start()
            for p in range(pieces):
                edge_tok_copy(side, p, target).start()

    @pl.loop(0, pieces)
    def _(p):
        at = pl.ds(pl.multiple_of(p * width, LANES), width)
        for b in range(ntp):
            part[p, b * tp_cols:(b + 1) * tp_cols, :] = lax.dot_general(
                cots[b], tok[:, at], (((0,), (0,)), ((), ())), preferred_element_type=F32).astype(BF16)

    sum_step(0)

    @pl.loop(1, n)
    def _(tau):
        weight_step(tau)
        sum_step(tau)

    @pl.loop(1, pieces)
    def _(p):
        vote(p - 1)
        @pl.when(p > 1)
        def _():
            count(p - 2)
        @pl.loop(1, n)
        def _(j):
            sum_step(p * (n - 1) + j)

    vote(pieces - 1)
    if pieces > 1:
        count(pieces - 2)
    project()
    count(pieces - 1)
    for off in range(1, ntp):
        half_copy(off).wait_recv()
    total = halves[0]
    for b in range(1, ntp):
        total = total + halves[b]
    proj[...] = total.astype(BF16)

    @pl.loop(0, pieces)
    def _(p):
        finish(p)

    for off in range(1, ntp):
        cot_copy(off).wait_send()
        half_copy(off).wait_send()

    @pl.loop(0, pieces)
    def _(p):
        for off in range(1, nrep):
            vote_copy(p, off).wait_send()
            tally_copy(p, off).wait_send()
        for k in range(n):
            @pl.when((k > z) & (z > 0))
            def _():
                sum_copy(right_buf, p, k, rs_s, rs_r, z).wait_send()
            @pl.when((k < z) & (z < n - 1))
            def _():
                sum_copy(left_buf, p, k, ls_s, ls_r, z).wait_send()
    for side, edge in ((0, 0), (1, n - 1)):
        @pl.when(z == edge)
        def _():
            edge_cot_copy(side, z).wait_send()
            for p in range(pieces):
                edge_tok_copy(side, p, z).wait_send()
    for shard in range(n):
        @pl.when((shard <= z) & (z + 1 < n))
        def _():
            weight_line(False, shard, wrs, wrr, z).wait_send()
        @pl.when((shard >= z) & (z > 0))
        def _():
            weight_line(False, shard, wls, wlr, z).wait_send()
        @pl.when(shard != z)
        def _():
            for off in range(1, nrep):
                weight_plane(shard, off).wait_send()


def shards(n, nrep, ntp, tokens, cotangent, weight, momentum):
    held, half = tokens.shape
    rows, cols = weight.shape[0], weight.shape[0] * n
    pieces = max(1, min(8, half // (LANES * nrep)))
    width = half // pieces
    share = width // nrep
    scale = 1.0 / math.sqrt(held * n)
    dma = pltpu.SemaphoreType.DMA
    vmem = pl.BlockSpec(memory_space=pltpu.VMEM)
    projected, update, gradient = pl.pallas_call(
        functools.partial(step, (n, nrep, ntp, pieces, rows, width, share), scale),
        out_shape=(
            jax.ShapeDtypeStruct((held, cols), BF16),
            jax.ShapeDtypeStruct((rows, half), BF16),
            jax.ShapeDtypeStruct((rows, half), BF16),
        ),
        in_specs=[vmem] * 4,
        out_specs=(vmem,) * 3,
        scratch_shapes=[
            pltpu.VMEM((pieces, cols, width), BF16),
            pltpu.VMEM((pieces, cols, width), BF16),
            pltpu.VMEM((pieces, cols, width), BF16),
            pltpu.VMEM((cols, half), BF16),
            pltpu.VMEM((ntp,) + cotangent.shape, BF16),
            pltpu.VMEM((ntp, held, cols), F32),
            pltpu.VMEM((pieces, nrep, rows, share), BF16),
            pltpu.VMEM((pieces, nrep, rows, share), BF16),
            pltpu.VMEM((pieces, nrep, rows, share), BF16),
            pltpu.VMEM((2, pieces, held, width), BF16),
            pltpu.VMEM((2, ntp) + cotangent.shape, BF16),
        ]
        + [dma((pieces, n))] * 4
        + [dma((n,))] * 4
        + [dma((n, nrep))] * 2
        + [dma((pieces, nrep))] * 4
        + [dma((ntp,))] * 4
        + [dma((2, pieces + 1))] * 2,
        compiler_params=pltpu.CompilerParams(
            collective_id=0, has_side_effects=True, vmem_limit_bytes=60 * 1024 * 1024
        ),
    )(tokens, cotangent, weight, momentum)
    renewed = BETA_TWO * momentum.astype(F32) + (1.0 - BETA_TWO) * gradient.astype(F32)[None]
    return (projected, update.astype(F32), renewed)


def solution(mesh):
    sizes = dict(mesh.shape)
    return jax.shard_map(
        functools.partial(shards, sizes["fsdp"], sizes["rep"], sizes["tp"]),
        mesh=mesh,
        in_specs=(
            P(("rep", "fsdp"), "tp"),
            P(("rep", "fsdp"), "tp"),
            P("fsdp", "tp"),
            P("rep", "fsdp", "tp"),
        ),
        out_specs=(P(("rep", "fsdp"), None), P("fsdp", "tp"), P("rep", "fsdp", "tp")),
        check_vma=False,
    )
```

```python
import functools
import math

import jax
import jax.numpy as jnp
from jax import lax
from jax.experimental import pallas as pl
from jax.experimental.pallas import tpu as pltpu
from jax.sharding import PartitionSpec as P

BETA_ONE = 0.9
BETA_TWO = 0.99
SOFT_WIDTH = 0.25
LANES = 128
LAG = 4
MESH = pl.DeviceIdType.MESH
F32 = jnp.float32
BF16 = jnp.bfloat16


def step(dims, scale, tok, cot, wgt, mom, proj, upd, grad, *scratch):
    (n, nrep, ntp, pieces, rows, width, share) = dims
    (right_buf, left_buf, part, weights, cots, halves, signs, votes, tally, edge_toks, edge_cots, cots_t) = scratch[:12]
    (rs_s, rs_r, ls_s, ls_r, wrs, wrr, wls, wlr, wps, wpr, vs, vr, ts, tr, cs, cr, hs, hr, es, er) = scratch[12:]
    z, me, t = lax.axis_index("fsdp"), lax.axis_index("rep"), lax.axis_index("tp")
    quarter = weights.shape[1] // nrep
    tp_cols = cot.shape[1]

    def to(axis, at):
        return dict(device_id={axis: at}, device_id_type=MESH)

    def other(off, size, at):
        return lax.rem(at + off, size)

    barrier = pltpu.get_barrier_semaphore()
    for axis, at, size in (("tp", t, ntp), ("rep", me, nrep)):
        for off in range(1, size):
            pl.semaphore_signal(barrier, inc=1, **to(axis, other(off, size, at)))
    for off in (1, n - 1):
        pl.semaphore_signal(barrier, inc=1, **to("fsdp", other(off, n, z)))
    pl.semaphore_wait(barrier, ntp + nrep)

    def cot_copy(off):
        return pltpu.make_async_remote_copy(
            cot, cots.at[t], cs.at[off], cr.at[off], **to("tp", other(off, ntp, t)))

    def half_copy(off):
        return pltpu.make_async_remote_copy(
            halves.at[t], halves.at[t], hs.at[off], hr.at[off], **to("tp", other(off, ntp, t)))

    def weight_slot(shard, rep):
        return weights.at[pl.ds(pl.multiple_of(shard * rows, rows), rows),
                          pl.ds(pl.multiple_of(rep * quarter, LANES), quarter)]

    def weight_line(own, shard, send, recv, target):
        slot = weight_slot(shard, me)
        source = wgt.at[:, pl.ds(pl.multiple_of(me * quarter, LANES), quarter)] if own else slot
        return pltpu.make_async_remote_copy(
            source, slot, send.at[shard], recv.at[shard], **to("fsdp", target))

    def weight_plane(shard, off):
        slot = weight_slot(shard, me)
        return pltpu.make_async_remote_copy(
            slot, slot, wps.at[shard, off], wpr.at[shard, off], **to("rep", other(off, nrep, me)))

    def sum_copy(buf, p, k, send, recv, target):
        slot = buf.at[p, pl.ds(pl.multiple_of(k * rows, rows), rows), :]
        return pltpu.make_async_remote_copy(slot, slot, send.at[p, k], recv.at[p, k], **to("fsdp", target))

    def edge_cot_copy(side, target):
        return pltpu.make_async_remote_copy(
            cots, edge_cots.at[side], es.at[side, pieces], er.at[side, pieces], **to("fsdp", target))

    def edge_tok_copy(side, p, target):
        at = pl.ds(pl.multiple_of(p * width, LANES), width)
        return pltpu.make_async_remote_copy(
            tok.at[:, at], edge_toks.at[side, p], es.at[side, p], er.at[side, p], **to("fsdp", target))

    def vote_copy(p, off):
        return pltpu.make_async_remote_copy(
            signs.at[p, other(off, nrep, me)], votes.at[p, me], vs.at[p, off], vr.at[p, off],
            **to("rep", other(off, nrep, me)))

    def tally_copy(p, off):
        return pltpu.make_async_remote_copy(
            tally.at[p, me], tally.at[p, me], ts.at[p, off], tr.at[p, off],
            **to("rep", other(off, nrep, me)))

    def weight_step(i, first=False):
        for send, recv, shard, target, ok in (
            (wrs, wrr, z - i, z + 1, z + 1 < n), (wls, wlr, z + i, z - 1, z > 0)):
            here = (shard >= 0) & (shard < n)
            if not first:
                @pl.when(here)
                def _():
                    weight_line(False, shard, send, recv, z).wait_recv()
            @pl.when(here & ok)
            def _():
                weight_line(first, shard, send, recv, target).start()
            if not first:
                @pl.when(here)
                def _():
                    for off in range(1, nrep):
                        weight_plane(shard, off).start()

    def turn(source, slot):
        for b in range(ntp):
            cots_t[slot, b * tp_cols:(b + 1) * tp_cols, :] = source[b].T

    def sum_step(tau):
        for side, buf, send, recv, depth, toward in (
            (0, right_buf, rs_s, rs_r, z, z + 1), (1, left_buf, ls_s, ls_r, n - 1 - z, z - 1)):
            i = tau - LAG * depth
            p, j = i // (n - 1), lax.rem(jnp.maximum(i, 0), n - 1)
            k = j if side else n - 1 - j
            inside = (i >= 0) & (i < pieces * (n - 1))
            ahead = (k < z) if side else (k > z)
            @pl.when(inside & (depth == 1) & (j == 0))
            def _():
                @pl.when(p == 0)
                def _():
                    edge_cot_copy(side, z).wait_recv()
                    turn(edge_cots.at[side], side)
                edge_tok_copy(side, p, z).wait_recv()
                buf[p] = jnp.dot(cots_t[side], edge_toks[side, p], preferred_element_type=F32).astype(BF16)
            @pl.when(inside & (ahead | (k == z)) & (depth > 1))
            def _():
                sum_copy(buf, p, k, send, recv, z).wait_recv()
            rk = pl.ds(pl.multiple_of(k * rows, rows), rows)
            @pl.when(inside & ahead & (depth > 0))
            def _():
                buf[p, rk, :] = (buf[p, rk, :].astype(F32) + part[p, rk, :].astype(F32)).astype(BF16)
                sum_copy(buf, p, k, send, recv, toward).start()

    own_rows = pl.ds(pl.multiple_of(z * rows, rows), rows)

    def vote(p):
        for s in range(nrep):
            cut = pl.ds(s * share, share)
            at = pl.ds(pl.multiple_of(p * width + s * share, LANES), share)
            g = (part[p, own_rows, cut].astype(F32) + right_buf[p, own_rows, cut].astype(F32)
                 + left_buf[p, own_rows, cut].astype(F32)) * scale
            grad[:, at] = g.astype(BF16)
            blended = BETA_ONE * mom[0, :, at].astype(F32) + (1.0 - BETA_ONE) * g
            signs[p, s] = jnp.clip(blended / SOFT_WIDTH, -1.0, 1.0).astype(BF16)
        for off in range(1, nrep):
            vote_copy(p, off).start()

    def count(p):
        total = signs[p, me].astype(F32)
        for off in range(1, nrep):
            vote_copy(p, off).wait_recv()
            total = total + votes[p, other(nrep - off, nrep, me)].astype(F32)
        tally[p, me] = jnp.clip(total, -1.0, 1.0).astype(BF16)
        for off in range(1, nrep):
            tally_copy(p, off).start()

    def finish(p):
        for off in range(1, nrep):
            tally_copy(p, off).wait_recv()
        for s in range(nrep):
            upd[:, pl.ds(pl.multiple_of(p * width + s * share, LANES), share)] = tally[p, s]

    def project():
        for i in range(n):
            for shard in ((z - i, z + i) if i > 0 else ()):
                @pl.when((shard >= 0) & (shard < n))
                def _():
                    for off in range(1, nrep):
                        weight_plane(shard, off).wait_recv()
        halves[t] = jnp.zeros(halves.shape[1:], F32)
        @pl.loop(0, pieces)
        def _(p):
            at = pl.ds(pl.multiple_of(p * width, LANES), width)
            halves[t] += lax.dot_general(
                tok[:, at], weights[:, at], (((1,), (1,)), ((), ())), preferred_element_type=F32)
        for off in range(1, ntp):
            half_copy(off).start()

    for off in range(1, ntp):
        cot_copy(off).start()
    weight_step(0, True)
    weights[own_rows, :] = wgt[...]
    cots[t] = cot[...]
    for buf, edge in ((right_buf, 0), (left_buf, n - 1)):
        @pl.when(z == edge)
        def _():
            buf[:, edge * rows:(edge + 1) * rows, :] = jnp.zeros((pieces, rows, width), BF16)
    for off in range(1, ntp):
        cot_copy(off).wait_recv()
    for side, edge, target in ((0, 0, z + 1), (1, n - 1, z - 1)):
        @pl.when(z == edge)
        def _():
            edge_cot_copy(side, target).start()
            for p in range(pieces):
                edge_tok_copy(side, p, target).start()

    turn(cots, 2)

    @pl.loop(0, pieces)
    def _(p):
        at = pl.ds(pl.multiple_of(p * width, LANES), width)
        part[p] = jnp.dot(cots_t[2], tok[:, at], preferred_element_type=F32).astype(BF16)

    sum_step(0)

    @pl.loop(1, n)
    def _(tau):
        weight_step(tau)
        sum_step(tau)

    @pl.loop(n, LAG * (n - 1) + 1)
    def _(tau):
        sum_step(tau)

    @pl.loop(1, pieces)
    def _(p):
        vote(p - 1)
        @pl.when(p > 1)
        def _():
            count(p - 2)
        @pl.loop(1, n)
        def _(j):
            sum_step((p + LAG - 1) * (n - 1) + j)

    vote(pieces - 1)
    if pieces > 1:
        count(pieces - 2)
    project()
    count(pieces - 1)
    for off in range(1, ntp):
        half_copy(off).wait_recv()
    total = halves[0]
    for b in range(1, ntp):
        total = total + halves[b]
    proj[...] = total.astype(BF16)

    @pl.loop(0, pieces)
    def _(p):
        finish(p)

    for off in range(1, ntp):
        cot_copy(off).wait_send()
        half_copy(off).wait_send()

    @pl.loop(0, pieces)
    def _(p):
        for off in range(1, nrep):
            vote_copy(p, off).wait_send()
            tally_copy(p, off).wait_send()
        for k in range(n):
            @pl.when((k > z) & (z > 0))
            def _():
                sum_copy(right_buf, p, k, rs_s, rs_r, z).wait_send()
            @pl.when((k < z) & (z < n - 1))
            def _():
                sum_copy(left_buf, p, k, ls_s, ls_r, z).wait_send()
    for side, edge in ((0, 0), (1, n - 1)):
        @pl.when(z == edge)
        def _():
            edge_cot_copy(side, z).wait_send()
            for p in range(pieces):
                edge_tok_copy(side, p, z).wait_send()
    for shard in range(n):
        @pl.when((shard <= z) & (z + 1 < n))
        def _():
            weight_line(False, shard, wrs, wrr, z).wait_send()
        @pl.when((shard >= z) & (z > 0))
        def _():
            weight_line(False, shard, wls, wlr, z).wait_send()
        @pl.when(shard != z)
        def _():
            for off in range(1, nrep):
                weight_plane(shard, off).wait_send()


def shards(n, nrep, ntp, tokens, cotangent, weight, momentum):
    held, half = tokens.shape
    rows, cols = weight.shape[0], weight.shape[0] * n
    pieces = max(1, min(8, half // (LANES * nrep)))
    width = half // pieces
    share = width // nrep
    scale = 1.0 / math.sqrt(held * n)
    dma = pltpu.SemaphoreType.DMA
    vmem = pl.BlockSpec(memory_space=pltpu.VMEM)
    projected, update, gradient = pl.pallas_call(
        functools.partial(step, (n, nrep, ntp, pieces, rows, width, share), scale),
        out_shape=(
            jax.ShapeDtypeStruct((held, cols), BF16),
            jax.ShapeDtypeStruct((rows, half), BF16),
            jax.ShapeDtypeStruct((rows, half), BF16),
        ),
        in_specs=[vmem] * 4,
        out_specs=(vmem,) * 3,
        scratch_shapes=[
            pltpu.VMEM((pieces, cols, width), BF16),
            pltpu.VMEM((pieces, cols, width), BF16),
            pltpu.VMEM((pieces, cols, width), BF16),
            pltpu.VMEM((cols, half), BF16),
            pltpu.VMEM((ntp,) + cotangent.shape, BF16),
            pltpu.VMEM((ntp, held, cols), F32),
            pltpu.VMEM((pieces, nrep, rows, share), BF16),
            pltpu.VMEM((pieces, nrep, rows, share), BF16),
            pltpu.VMEM((pieces, nrep, rows, share), BF16),
            pltpu.VMEM((2, pieces, held, width), BF16),
            pltpu.VMEM((2, ntp) + cotangent.shape, BF16),
            pltpu.VMEM((3, cols, held), BF16),
        ]
        + [dma((pieces, n))] * 4
        + [dma((n,))] * 4
        + [dma((n, nrep))] * 2
        + [dma((pieces, nrep))] * 4
        + [dma((ntp,))] * 4
        + [dma((2, pieces + 1))] * 2,
        compiler_params=pltpu.CompilerParams(
            collective_id=0, has_side_effects=True, vmem_limit_bytes=60 * 1024 * 1024
        ),
    )(tokens, cotangent, weight, momentum)
    renewed = BETA_TWO * momentum.astype(F32) + (1.0 - BETA_TWO) * gradient.astype(F32)[None]
    return (projected, update.astype(F32), renewed)


def solution(mesh):
    sizes = dict(mesh.shape)
    return jax.shard_map(
        functools.partial(shards, sizes["fsdp"], sizes["rep"], sizes["tp"]),
        mesh=mesh,
        in_specs=(
            P(("rep", "fsdp"), "tp"),
            P(("rep", "fsdp"), "tp"),
            P("fsdp", "tp"),
            P("rep", "fsdp", "tp"),
        ),
        out_specs=(P(("rep", "fsdp"), None), P("fsdp", "tp"), P("rep", "fsdp", "tp")),
        check_vma=False,
    )
```

```python
import functools
import math

import jax
import jax.numpy as jnp
from jax import lax
from jax.experimental import pallas as pl
from jax.experimental.pallas import tpu as pltpu
from jax.sharding import PartitionSpec as P

BETA_ONE = 0.9
BETA_TWO = 0.99
SOFT_WIDTH = 0.25
LANES = 128
LAG = 4
MESH = pl.DeviceIdType.MESH
F32 = jnp.float32
BF16 = jnp.bfloat16


def step(dims, scale, tok, cot, wgt, mom, proj, upd, grad, *scratch):
    (n, nrep, ntp, pieces, rows, width, share) = dims
    (right_buf, left_buf, part, weights, cots, halves, signs, votes, tally, edge_toks, edge_cots, cots_t) = scratch[:12]
    (rs_s, rs_r, ls_s, ls_r, wrs, wrr, wls, wlr, wps, wpr, vs, vr, ts, tr, cs, cr, hs, hr, es, er) = scratch[12:]
    z, me, t = lax.axis_index("fsdp"), lax.axis_index("rep"), lax.axis_index("tp")
    quarter = weights.shape[1] // nrep
    tp_cols = cot.shape[1]

    def to(axis, at):
        return dict(device_id={axis: at}, device_id_type=MESH)

    def other(off, size, at):
        return lax.rem(at + off, size)

    barrier = pltpu.get_barrier_semaphore()
    for axis, at, size in (("tp", t, ntp), ("rep", me, nrep)):
        for off in range(1, size):
            pl.semaphore_signal(barrier, inc=1, **to(axis, other(off, size, at)))
    for off in (1, n - 1):
        pl.semaphore_signal(barrier, inc=1, **to("fsdp", other(off, n, z)))
    pl.semaphore_wait(barrier, ntp + nrep)

    def cot_copy(off):
        return pltpu.make_async_remote_copy(
            cot, cots.at[t], cs.at[off], cr.at[off], **to("tp", other(off, ntp, t)))

    def half_copy(off):
        return pltpu.make_async_remote_copy(
            halves.at[t], halves.at[t], hs.at[off], hr.at[off], **to("tp", other(off, ntp, t)))

    def weight_slot(shard, rep):
        return weights.at[pl.ds(pl.multiple_of(shard * rows, rows), rows),
                          pl.ds(pl.multiple_of(rep * quarter, LANES), quarter)]

    def weight_line(own, shard, send, recv, target):
        slot = weight_slot(shard, me)
        source = wgt.at[:, pl.ds(pl.multiple_of(me * quarter, LANES), quarter)] if own else slot
        return pltpu.make_async_remote_copy(
            source, slot, send.at[shard], recv.at[shard], **to("fsdp", target))

    def weight_plane(shard, off):
        slot = weight_slot(shard, me)
        return pltpu.make_async_remote_copy(
            slot, slot, wps.at[shard, off], wpr.at[shard, off], **to("rep", other(off, nrep, me)))

    def sum_copy(buf, p, k, send, recv, target):
        slot = buf.at[p, pl.ds(pl.multiple_of(k * rows, rows), rows), :]
        return pltpu.make_async_remote_copy(slot, slot, send.at[p, k], recv.at[p, k], **to("fsdp", target))

    def edge_cot_copy(side, target):
        return pltpu.make_async_remote_copy(
            cots, edge_cots.at[side], es.at[side, pieces], er.at[side, pieces], **to("fsdp", target))

    def edge_tok_copy(side, p, target):
        at = pl.ds(pl.multiple_of(p * width, LANES), width)
        return pltpu.make_async_remote_copy(
            tok.at[:, at], edge_toks.at[side, p], es.at[side, p], er.at[side, p], **to("fsdp", target))

    def vote_copy(p, off):
        return pltpu.make_async_remote_copy(
            signs.at[p, other(off, nrep, me)], votes.at[p, me], vs.at[p, off], vr.at[p, off],
            **to("rep", other(off, nrep, me)))

    def tally_copy(p, off):
        return pltpu.make_async_remote_copy(
            tally.at[p, me], tally.at[p, me], ts.at[p, off], tr.at[p, off],
            **to("rep", other(off, nrep, me)))

    def weight_step(i, first=False):
        for send, recv, shard, target, ok in (
            (wrs, wrr, z - i, z + 1, z + 1 < n), (wls, wlr, z + i, z - 1, z > 0)):
            here = (shard >= 0) & (shard < n)
            if not first:
                @pl.when(here)
                def _():
                    weight_line(False, shard, send, recv, z).wait_recv()
            @pl.when(here & ok)
            def _():
                weight_line(first, shard, send, recv, target).start()
            if not first:
                @pl.when(here)
                def _():
                    for off in range(1, nrep):
                        weight_plane(shard, off).start()

    def turn(source, slot):
        for b in range(ntp):
            cots_t[slot, b * tp_cols:(b + 1) * tp_cols, :] = source[b].T

    def sum_step(tau):
        for side, buf, send, recv, depth, toward in (
            (0, right_buf, rs_s, rs_r, z, z + 1), (1, left_buf, ls_s, ls_r, n - 1 - z, z - 1)):
            i = tau - LAG * depth
            p, j = i // (n - 1), lax.rem(jnp.maximum(i, 0), n - 1)
            k = j if side else n - 1 - j
            inside = (i >= 0) & (i < pieces * (n - 1))
            ahead = (k < z) if side else (k > z)
            @pl.when(inside & (depth == 1) & (j == 0))
            def _():
                @pl.when(p == 0)
                def _():
                    edge_cot_copy(side, z).wait_recv()
                    turn(edge_cots.at[side], side)
                edge_tok_copy(side, p, z).wait_recv()
                buf[p] = jnp.dot(cots_t[side], edge_toks[side, p], preferred_element_type=F32).astype(BF16)
            @pl.when(inside & (ahead | (k == z)) & (depth > 1))
            def _():
                sum_copy(buf, p, k, send, recv, z).wait_recv()
            rk = pl.ds(pl.multiple_of(k * rows, rows), rows)
            @pl.when(inside & ahead & (depth > 0))
            def _():
                buf[p, rk, :] = (buf[p, rk, :].astype(F32) + part[p, rk, :].astype(F32)).astype(BF16)
                sum_copy(buf, p, k, send, recv, toward).start()

    own_rows = pl.ds(pl.multiple_of(z * rows, rows), rows)

    def vote(p):
        for s in range(nrep):
            cut = pl.ds(s * share, share)
            at = pl.ds(pl.multiple_of(p * width + s * share, LANES), share)
            g = (part[p, own_rows, cut].astype(F32) + right_buf[p, own_rows, cut].astype(F32)
                 + left_buf[p, own_rows, cut].astype(F32)) * scale
            grad[:, at] = g.astype(BF16)
            blended = BETA_ONE * mom[0, :, at].astype(F32) + (1.0 - BETA_ONE) * g
            signs[p, s] = jnp.clip(blended / SOFT_WIDTH, -1.0, 1.0).astype(BF16)
        for off in range(1, nrep):
            vote_copy(p, off).start()

    def count(p):
        total = signs[p, me].astype(F32)
        for off in range(1, nrep):
            vote_copy(p, off).wait_recv()
            total = total + votes[p, other(nrep - off, nrep, me)].astype(F32)
        tally[p, me] = jnp.clip(total, -1.0, 1.0).astype(BF16)
        for off in range(1, nrep):
            tally_copy(p, off).start()

    def finish(p):
        for off in range(1, nrep):
            tally_copy(p, off).wait_recv()
        for s in range(nrep):
            upd[:, pl.ds(pl.multiple_of(p * width + s * share, LANES), share)] = tally[p, s]

    def project():
        for i in range(n):
            for shard in ((z - i, z + i) if i > 0 else ()):
                @pl.when((shard >= 0) & (shard < n))
                def _():
                    for off in range(1, nrep):
                        weight_plane(shard, off).wait_recv()
        halves[t] = jnp.zeros(halves.shape[1:], F32)
        @pl.loop(0, pieces)
        def _(p):
            at = pl.ds(pl.multiple_of(p * width, LANES), width)
            halves[t] += lax.dot_general(
                tok[:, at], weights[:, at], (((1,), (1,)), ((), ())), preferred_element_type=F32)
        for off in range(1, ntp):
            half_copy(off).start()

    for off in range(1, ntp):
        cot_copy(off).start()
    weight_step(0, True)
    weights[own_rows, :] = wgt[...]
    cots[t] = cot[...]
    for buf, edge in ((right_buf, 0), (left_buf, n - 1)):
        @pl.when(z == edge)
        def _():
            buf[:, edge * rows:(edge + 1) * rows, :] = jnp.zeros((pieces, rows, width), BF16)
    for off in range(1, ntp):
        cot_copy(off).wait_recv()
    for side, edge, target in ((0, 0, z + 1), (1, n - 1, z - 1)):
        @pl.when(z == edge)
        def _():
            edge_cot_copy(side, target).start()
            for p in range(pieces):
                edge_tok_copy(side, p, target).start()

    turn(cots, 2)

    @pl.loop(0, pieces)
    def _(p):
        at = pl.ds(pl.multiple_of(p * width, LANES), width)
        part[p] = jnp.dot(cots_t[2], tok[:, at], preferred_element_type=F32).astype(BF16)

    sum_step(0)

    @pl.loop(1, n)
    def _(tau):
        weight_step(tau)
        sum_step(tau)

    @pl.loop(n, LAG * (n - 1) + 1)
    def _(tau):
        sum_step(tau)

    @pl.loop(1, pieces)
    def _(p):
        vote(p - 1)
        @pl.when(p > 2)
        def _():
            count(p - 3)
        @pl.loop(1, n)
        def _(j):
            sum_step((p + LAG - 1) * (n - 1) + j)

    vote(pieces - 1)
    for p in range(max(0, pieces - 3), pieces - 1):
        count(p)
    project()
    count(pieces - 1)
    for off in range(1, ntp):
        half_copy(off).wait_recv()
    total = halves[0]
    for b in range(1, ntp):
        total = total + halves[b]
    proj[...] = total.astype(BF16)

    @pl.loop(0, pieces)
    def _(p):
        finish(p)

    for off in range(1, ntp):
        cot_copy(off).wait_send()
        half_copy(off).wait_send()

    @pl.loop(0, pieces)
    def _(p):
        for off in range(1, nrep):
            vote_copy(p, off).wait_send()
            tally_copy(p, off).wait_send()
        for k in range(n):
            @pl.when((k > z) & (z > 0))
            def _():
                sum_copy(right_buf, p, k, rs_s, rs_r, z).wait_send()
            @pl.when((k < z) & (z < n - 1))
            def _():
                sum_copy(left_buf, p, k, ls_s, ls_r, z).wait_send()
    for side, edge in ((0, 0), (1, n - 1)):
        @pl.when(z == edge)
        def _():
            edge_cot_copy(side, z).wait_send()
            for p in range(pieces):
                edge_tok_copy(side, p, z).wait_send()
    for shard in range(n):
        @pl.when((shard <= z) & (z + 1 < n))
        def _():
            weight_line(False, shard, wrs, wrr, z).wait_send()
        @pl.when((shard >= z) & (z > 0))
        def _():
            weight_line(False, shard, wls, wlr, z).wait_send()
        @pl.when(shard != z)
        def _():
            for off in range(1, nrep):
                weight_plane(shard, off).wait_send()


def shards(n, nrep, ntp, tokens, cotangent, weight, momentum):
    held, half = tokens.shape
    rows, cols = weight.shape[0], weight.shape[0] * n
    pieces = max(1, min(8, half // (LANES * nrep)))
    width = half // pieces
    share = width // nrep
    scale = 1.0 / math.sqrt(held * n)
    dma = pltpu.SemaphoreType.DMA
    vmem = pl.BlockSpec(memory_space=pltpu.VMEM)
    projected, update, gradient = pl.pallas_call(
        functools.partial(step, (n, nrep, ntp, pieces, rows, width, share), scale),
        out_shape=(
            jax.ShapeDtypeStruct((held, cols), BF16),
            jax.ShapeDtypeStruct((rows, half), BF16),
            jax.ShapeDtypeStruct((rows, half), BF16),
        ),
        in_specs=[vmem] * 4,
        out_specs=(vmem,) * 3,
        scratch_shapes=[
            pltpu.VMEM((pieces, cols, width), BF16),
            pltpu.VMEM((pieces, cols, width), BF16),
            pltpu.VMEM((pieces, cols, width), BF16),
            pltpu.VMEM((cols, half), BF16),
            pltpu.VMEM((ntp,) + cotangent.shape, BF16),
            pltpu.VMEM((ntp, held, cols), F32),
            pltpu.VMEM((pieces, nrep, rows, share), BF16),
            pltpu.VMEM((pieces, nrep, rows, share), BF16),
            pltpu.VMEM((pieces, nrep, rows, share), BF16),
            pltpu.VMEM((2, pieces, held, width), BF16),
            pltpu.VMEM((2, ntp) + cotangent.shape, BF16),
            pltpu.VMEM((3, cols, held), BF16),
        ]
        + [dma((pieces, n))] * 4
        + [dma((n,))] * 4
        + [dma((n, nrep))] * 2
        + [dma((pieces, nrep))] * 4
        + [dma((ntp,))] * 4
        + [dma((2, pieces + 1))] * 2,
        compiler_params=pltpu.CompilerParams(
            collective_id=0, has_side_effects=True, vmem_limit_bytes=60 * 1024 * 1024
        ),
    )(tokens, cotangent, weight, momentum)
    renewed = BETA_TWO * momentum.astype(F32) + (1.0 - BETA_TWO) * gradient.astype(F32)[None]
    return (projected, update.astype(F32), renewed)


def solution(mesh):
    sizes = dict(mesh.shape)
    return jax.shard_map(
        functools.partial(shards, sizes["fsdp"], sizes["rep"], sizes["tp"]),
        mesh=mesh,
        in_specs=(
            P(("rep", "fsdp"), "tp"),
            P(("rep", "fsdp"), "tp"),
            P("fsdp", "tp"),
            P("rep", "fsdp", "tp"),
        ),
        out_specs=(P(("rep", "fsdp"), None), P("fsdp", "tp"), P("rep", "fsdp", "tp")),
        check_vma=False,
    )
```
